32 devices in a mesh: dp: 8 (over z, y), fsdp: 4 (over x, core).
Axes of the slice: x: 2, y: 2, z: 4, core: 2. Of those that a mesh axis runs over, the one named last changes fastest.
Arguments:
- keys: bfloat16 [256, 8, 896], P(('dp', 'fsdp')), may hold values from -8 to 8
- residual: bfloat16 [256, 8, 896], P(('dp', 'fsdp')), may hold values from -6 to 6
- se_reduce: bfloat16 [896, 224], P('fsdp'), may hold values from -0.625 to 0.625
- se_expand: bfloat16 [896, 224], P('fsdp'), may hold values from -1.25 to 1.25
- conv_weight: bfloat16 [3, 896, 896], P(None, 'fsdp'), may hold values from -0.1875 to 0.1875
- bn_gain: float32 [896], replicated, may hold values from 0.1 to 1.9
- bn_bias: float32 [896], replicated, may hold values from -3 to 3
- shuffle: int32 [256], P(('dp', 'fsdp')), may hold values from 0 to 63, as said below
- unshuffle: int32 [256], P(('dp', 'fsdp')), may hold values from 0 to 63, as said below
Outputs:
- encoded: bfloat16 [256, 8, 896], P(('dp', 'fsdp'))
The draws below stay inside these ranges and needn't reach their ends.
Inputs may be any that keep to these rules, and one draw needn't show every extreme that they name: `shuffle`: A permutation of the 64 positions within each group of devices sharing an fsdp index (positions ordered by dp index, then by image); each device sends exactly 1 of its images to every device of its group. `unshuffle`: the inverse of shuffle within each group.
All inputs are finite; a program needn't handle non-finite values.
Results may differ from the reference program's by a relative error of at most 0.013.
Values may be sent and summed in bfloat16 or wider, within the bound.
A program may use at most 64 MiB of HBM per device.

```python
import jax
import jax.numpy as jnp
from jax import lax

C = 896
S = 224
PIX = 8
LAYERS = 3
PER_PEER = 1
IMG_DEV = 8
BATCH = 256
N_DP = 8
N_FSDP = 4


def balanced_positions(key):
    first_key, second_key = jax.random.split(jax.random.fold_in(key, 7101))
    source_perm = jax.vmap(lambda one_key: jax.random.permutation(one_key, IMG_DEV))(jax.random.split(first_key, N_FSDP * N_DP))
    source_perm = source_perm.reshape(N_FSDP, N_DP, IMG_DEV).astype(jnp.int32)
    slot_perm = jax.vmap(lambda one_key: jax.random.permutation(one_key, IMG_DEV))(jax.random.split(second_key, N_FSDP * N_DP))
    slot_perm = slot_perm.reshape(N_FSDP, N_DP, IMG_DEV).astype(jnp.int32)
    target_device = source_perm // PER_PEER
    within_peer = source_perm % PER_PEER
    source_index = jnp.arange(N_DP, dtype=jnp.int32)[None, :, None]
    incoming = source_index * PER_PEER + within_peer
    fsdp_index = jnp.arange(N_FSDP, dtype=jnp.int32)[:, None, None]
    positions = target_device * IMG_DEV + slot_perm[fsdp_index, target_device, incoming]
    own_position = source_index * IMG_DEV + jnp.arange(IMG_DEV, dtype=jnp.int32)[None, None, :]
    fsdp_full = jnp.broadcast_to(fsdp_index, positions.shape)
    inverse = jnp.zeros((N_FSDP, N_DP * IMG_DEV), jnp.int32).at[fsdp_full, positions].set(jnp.broadcast_to(own_position, positions.shape))
    inverse = inverse.reshape(N_FSDP, N_DP, IMG_DEV)
    shuffle_flat = jnp.transpose(positions, (1, 0, 2)).reshape(BATCH)
    inverse_flat = jnp.transpose(inverse, (1, 0, 2)).reshape(BATCH)
    return (shuffle_flat, inverse_flat)


def draw_shuffle(key, part):
    return balanced_positions(key)[0]


def draw_unshuffle(key, part):
    return balanced_positions(key)[1]


def draw_keys(key, part):
    noise_key, scale_key = jax.random.split(jax.random.fold_in(key, 3301), 2)
    image_scale = jnp.exp(jax.random.uniform(scale_key, (BATCH, 1, 1), jnp.float32, jnp.log(0.3), jnp.log(3.0)))
    base = jax.random.normal(noise_key, (BATCH, PIX, C), jnp.float32)
    return jnp.clip(base * image_scale, -8.0, 8.0).astype(jnp.bfloat16)


def block_scale(stream_key, dims, pieces, least, largest):
    factor_of, own = 1.0, jax.random.fold_in(stream_key, 6)
    for position, parts in pieces:
        draws = jnp.exp(jax.random.uniform(jax.random.fold_in(own, position), (parts,), jnp.float32, least / len(pieces), largest / len(pieces)))
        factor_of = factor_of * jnp.repeat(draws, dims[position] // parts).reshape([-1 if axis == position else 1 for axis in range(len(dims))])
    return factor_of


def noise(key, dims, width, reach, cuts=(), held_as=jnp.bfloat16):
    values = width * jax.random.normal(key, dims, jnp.float32)
    if cuts:
        values = values * block_scale(key, dims, cuts, -0.22, 0.18)
    return jnp.clip(values, -reach, reach).astype(held_as)


def setup_inputs(seed: int = 0) -> dict:
    key_of = jax.random.split(jax.random.key(seed), 10)
    return {
        "keys": draw_keys(jax.random.fold_in(key_of[9], 71), 0),
        "residual": noise(key_of[1], (BATCH, PIX, C), 1.0, 6.0, ((0, 32),)),
        "se_reduce": noise(key_of[2], (C, S), (C // 9) ** -0.5, 0.625, ((0, 4),)),
        "se_expand": noise(key_of[3], (C, S), (S // 9) ** -0.5, 1.25, ((0, 4),)),
        "conv_weight": noise(key_of[4], (LAYERS, C, C), C ** -0.5, 0.1875, ((1, 4),)),
        "bn_gain": jnp.clip(1.0 + 0.18 * jax.random.normal(key_of[5], (C,), jnp.float32), 0.1, 1.9),
        "bn_bias": noise(key_of[6], (C,), 0.5, 3.0, (), jnp.float32),
        "shuffle": draw_shuffle(jax.random.fold_in(key_of[9], 71), 0),
        "unshuffle": draw_unshuffle(jax.random.fold_in(key_of[9], 71), 0),
    }


epsilon = 1e-05

def encode_block(batch_block, se_reduce, se_expand, conv_weight):
    images, positions, channels = batch_block.shape
    entry = batch_block.reshape(images * positions, channels)
    for layer in range(LAYERS - 1):
        entry = jax.nn.relu(jnp.dot(entry, conv_weight[layer], preferred_element_type=jnp.float32)).astype(jnp.bfloat16)
    entry = entry.reshape(images, positions, channels)
    pooled = lax.optimization_barrier(jnp.mean(entry, axis=1, dtype=jnp.float32)).astype(jnp.bfloat16)
    squeeze_act = jax.nn.relu(jnp.dot(pooled, se_reduce, preferred_element_type=jnp.float32)).astype(jnp.bfloat16)
    excite = jax.nn.sigmoid(jnp.dot(squeeze_act, se_expand.T, preferred_element_type=jnp.float32))
    scaled = (entry * excite[:, None, :]).astype(jnp.bfloat16)
    flat = scaled.reshape(-1, channels)
    projected = jnp.dot(flat, conv_weight[LAYERS - 1], preferred_element_type=jnp.float32)
    return projected.reshape(batch_block.shape)

def reference(keys, residual, se_reduce, se_expand, conv_weight, bn_gain, bn_bias, shuffle, unshuffle):
    channels = keys.shape[2]
    blocks = keys.reshape(N_DP, N_FSDP * IMG_DEV, PIX, channels)
    projected = lax.map(lambda part_block: encode_block(part_block, se_reduce, se_expand, conv_weight), blocks)
    projected = projected.reshape(N_DP, N_FSDP, IMG_DEV, PIX, channels)
    row_sums = lax.optimization_barrier(jnp.sum(projected, axis=3))
    square_sums = lax.optimization_barrier(jnp.sum(projected * projected, axis=3))

    def grouped(table):
        return jnp.transpose(table, (1, 0, 2, 3)).reshape(N_FSDP, N_DP * IMG_DEV, channels)
    anchor = jnp.transpose(unshuffle.reshape(N_DP, N_FSDP, IMG_DEV), (1, 0, 2)).reshape(N_FSDP, N_DP * IMG_DEV)
    anchor = anchor.astype(jnp.int32)
    sum_shuffled = jnp.take_along_axis(grouped(row_sums), anchor[:, :, None], axis=1)
    square_shuffled = jnp.take_along_axis(grouped(square_sums), anchor[:, :, None], axis=1)
    sum_device = lax.optimization_barrier(jnp.sum(sum_shuffled.reshape(N_FSDP, N_DP, IMG_DEV, channels), axis=2))
    square_device = lax.optimization_barrier(jnp.sum(square_shuffled.reshape(N_FSDP, N_DP, IMG_DEV, channels), axis=2))
    count = IMG_DEV * PIX
    mean_bn = sum_device / count
    var_bn = square_device / count - mean_bn * mean_bn
    inv_std = lax.rsqrt(var_bn + epsilon)
    target_device = (shuffle.reshape(N_DP, N_FSDP, IMG_DEV) // IMG_DEV).astype(jnp.int32)
    fsdp_index = jnp.arange(N_FSDP, dtype=jnp.int32)[None, :, None]
    mean_image = mean_bn[fsdp_index, target_device]
    scale_image = inv_std[fsdp_index, target_device] * bn_gain
    normed = ((projected - mean_image[:, :, :, None, :]) * scale_image[:, :, :, None, :] + bn_bias).astype(jnp.bfloat16)
    normed = lax.optimization_barrier(normed)
    normed = normed.reshape(keys.shape)
    encoded = jax.nn.relu(normed.astype(jnp.float32) + residual.astype(jnp.float32))
    return encoded.astype(jnp.bfloat16)
```

```python
import functools

import jax
import jax.numpy as jnp
from jax import lax
from jax.experimental import pallas as pl
from jax.experimental.pallas import tpu as pltpu
from jax.sharding import PartitionSpec as P

epsilon = 1e-05
lane = 128
MESH = pl.DeviceIdType.MESH


def project_rows(flat, weight_rows):
    return jnp.dot(
        flat,
        lax.all_gather(weight_rows, "fsdp", axis=0, tiled=True),
        preferred_element_type=jnp.float32,
    )


def encode_block(batch_block, reduce_full, expand_full, conv_weight):
    images, positions, channels = batch_block.shape
    layers = conv_weight.shape[0]
    flat = batch_block.reshape(images * positions, channels)
    for layer in range(layers - 1):
        flat = jax.nn.relu(project_rows(flat, conv_weight[layer])).astype(jnp.bfloat16)
    entry = flat.reshape(images, positions, channels)
    pooled = jnp.mean(entry, axis=1, dtype=jnp.float32).astype(jnp.bfloat16)
    squeeze_act = jax.nn.relu(
        jnp.dot(pooled, reduce_full, preferred_element_type=jnp.float32)
    ).astype(jnp.bfloat16)
    excite = jax.nn.sigmoid(
        lax.dot_general(
            squeeze_act, expand_full, (((1,), (1,)), ((), ())), preferred_element_type=jnp.float32
        )
    )
    scaled = (entry * excite[:, None, :]).astype(jnp.bfloat16).reshape(images * positions, channels)
    projected = project_rows(scaled, conv_weight[layers - 1])
    return projected.reshape(images, positions, channels)


def local_general(keys, residual, se_reduce, se_expand, conv_weight, bn_gain, bn_bias, shuffle, unshuffle):
    images, positions, channels = keys.shape
    count = images * positions
    reduce_full, expand_full = (
        lax.all_gather(se_reduce, "fsdp", axis=0, tiled=True),
        lax.all_gather(se_expand, "fsdp", axis=0, tiled=True),
    )
    send_order = jnp.argsort(shuffle)
    back_order = jnp.argsort(send_order)
    outgoing = jnp.take(keys, send_order, axis=0)
    arrived = lax.all_to_all(outgoing, "dp", split_axis=0, concat_axis=0, tiled=True)
    projected = encode_block(arrived, reduce_full, expand_full, conv_weight)
    row_sums = jnp.sum(projected, axis=(0, 1))
    square_sums = jnp.sum(projected * projected, axis=(0, 1))
    mean_rows = row_sums / count
    variance = square_sums / count - mean_rows * mean_rows
    scale_rows = lax.rsqrt(variance + epsilon) * bn_gain
    normed_here = ((projected - mean_rows) * scale_rows + bn_bias).astype(jnp.bfloat16)
    returned = lax.all_to_all(normed_here, "dp", split_axis=0, concat_axis=0, tiled=True)
    normed = jnp.take(returned, back_order, axis=0)
    encoded = jax.nn.relu(normed.astype(jnp.float32) + residual.astype(jnp.float32))
    return encoded.astype(jnp.bfloat16)


def fused_kernel(
    n_dp,
    images,
    positions,
    keys_ref,
    reduce_ref,
    expand_ref,
    weight_ref,
    gain_ref,
    bias_ref,
    shuffle_ref,
    out_ref,
    w,
    red,
    exp,
    kbuf,
    psend,
    precv,
    se_send,
    se_recv,
    hbuf,
    last_send,
    last_recv,
    table,
    sums_recv,
    stats,
    stats_recv,
    key_sem,
    weight_sem,
    layer_sem,
    se_sem,
    last_sem,
    sums_send_sem,
    sums_recv_sem,
    stats_send_sem,
    stats_recv_sem,
):
    me = lax.axis_index("dp")
    f = lax.axis_index("fsdp")
    x, c = f // 2, f % 2
    sibling = 2 * x + (1 - c)
    peer = 2 * (1 - x) + c
    layers, rows_dev, channels = weight_ref.shape
    half = 2 * rows_dev
    window = kbuf.shape[2]
    pad = window - half
    rows = images * positions
    own_lo = pl.multiple_of(x * (channels - window), lane)
    peer_lo = pl.multiple_of((1 - x) * (channels - window), lane)
    base = pl.multiple_of(x * pad + c * rows_dev, 16)

    keys_own = pltpu.make_async_copy(
        keys_ref.at[:, pl.ds(own_lo, window)], kbuf.at[x], key_sem.at[0]
    )
    keys_own.start()
    sources = [weight_ref.at[l] for l in range(layers)] + [reduce_ref, expand_ref]
    targets = [w.at[l] for l in range(layers)] + [red, exp]
    local_copies = []
    for s, (src, dst) in enumerate(zip(sources, targets)):
        copy = pltpu.make_async_copy(src, dst.at[pl.ds(base, rows_dev), :], weight_sem.at[0, s])
        copy.start()
        local_copies.append(copy)

    barrier = pltpu.get_barrier_semaphore()
    for other in (sibling, peer):
        pl.semaphore_signal(barrier, inc=1, device_id={"fsdp": other}, device_id_type=MESH)
    for k in range(1, n_dp):
        pl.semaphore_signal(
            barrier, inc=1, device_id={"dp": lax.rem(me + k, n_dp)}, device_id_type=MESH
        )
    pl.semaphore_wait(barrier, n_dp + 1)

    keys_peer = pltpu.make_async_remote_copy(
        src_ref=keys_ref.at[:, pl.ds(peer_lo, window)],
        dst_ref=kbuf.at[x],
        send_sem=key_sem.at[1],
        recv_sem=key_sem.at[2],
        device_id={"fsdp": peer},
        device_id_type=MESH,
    )
    keys_peer.start()
    shared = {}
    for s in (0, 1, layers, layers + 1, *range(2, layers)):
        shared[s] = pltpu.make_async_remote_copy(
            src_ref=sources[s],
            dst_ref=targets[s].at[pl.ds(base, rows_dev), :],
            send_sem=weight_sem.at[1, s],
            recv_sem=weight_sem.at[2, s],
            device_id={"fsdp": sibling},
            device_id_type=MESH,
        )
        shared[s].start()

    zero_lo = pl.multiple_of((1 - x) * half, 16)
    for l in range(layers):
        w[l, pl.ds(zero_lo, pad), :] = jnp.zeros((pad, channels), w.dtype)
    red[pl.ds(zero_lo, pad), :] = jnp.zeros((pad, red.shape[1]), red.dtype)
    exp[pl.ds(zero_lo, pad), :] = jnp.zeros((pad, exp.shape[1]), exp.dtype)

    def have_weights(s):
        local_copies[s].wait()
        shared[s].wait_recv()

    def to_peer(src, dst, sems):
        return pltpu.make_async_remote_copy(
            src_ref=src,
            dst_ref=dst,
            send_sem=sems.at[0],
            recv_sem=sems.at[1],
            device_id={"fsdp": peer},
            device_id_type=MESH,
        )

    keys_own.wait()
    keys_peer.wait_recv()
    pending = []
    entry = kbuf[...].reshape(2 * rows, window)
    for l in range(layers - 1):
        have_weights(l)
        theirs = jnp.dot(
            entry, w[l, :, pl.ds(peer_lo, window)], preferred_element_type=jnp.float32
        )
        psend[l] = theirs.astype(jnp.bfloat16)
        copy = to_peer(psend.at[l], precv.at[l], layer_sem.at[l])
        copy.start()
        mine = jnp.dot(
            entry, w[l, :, pl.ds(own_lo, window)], preferred_element_type=jnp.float32
        )
        copy.wait_recv()
        pending.append(copy)
        entry = jnp.maximum(mine + precv[l].astype(jnp.float32), 0.0).astype(jnp.bfloat16)

    have_weights(layers)
    have_weights(layers + 1)
    wide = entry.astype(jnp.float32).reshape(2 * images, positions, window)
    pooled = (jnp.sum(wide, axis=1) * (1.0 / positions)).astype(jnp.bfloat16)
    part = jnp.dot(pooled, red[...], preferred_element_type=jnp.float32)
    se_send[...] = part
    copy = to_peer(se_send, se_recv, se_sem)
    copy.start()
    copy.wait_recv()
    pending.append(copy)
    squeeze_act = jnp.maximum(part + se_recv[...], 0.0).astype(jnp.bfloat16)
    excite = jax.nn.sigmoid(
        lax.dot_general(
            squeeze_act, exp[...], (((1,), (1,)), ((), ())), preferred_element_type=jnp.float32
        )
    )
    scaled = (wide * excite[:, None, :]).astype(jnp.bfloat16)
    hbuf[...] = scaled.reshape(2, rows, window)

    have_weights(layers - 1)
    theirs = jnp.dot(hbuf[1 - x], w[layers - 1], preferred_element_type=jnp.float32)
    last_send[...] = theirs.astype(jnp.bfloat16)
    copy = to_peer(last_send, last_recv, last_sem)
    copy.start()
    mine = jnp.dot(hbuf[x], w[layers - 1], preferred_element_type=jnp.float32)
    copy.wait_recv()
    pending.append(copy)
    projected = (mine + last_recv[...].astype(jnp.float32)).reshape(images, positions, channels)

    image_sums = jnp.sum(projected, axis=1)
    image_squares = jnp.sum(projected * projected, axis=1)
    dests = [lax.div(shuffle_ref[i], images) for i in range(images)]
    device_row = lax.broadcasted_iota(jnp.int32, (n_dp, channels), 0)
    sums_table = jnp.zeros((n_dp, channels), jnp.float32)
    squares_table = jnp.zeros((n_dp, channels), jnp.float32)
    for i in range(images):
        hit = device_row == dests[i]
        sums_table = sums_table + jnp.where(hit, image_sums[i : i + 1], 0.0)
        squares_table = squares_table + jnp.where(hit, image_squares[i : i + 1], 0.0)
    table[:, 0, :] = sums_table
    table[:, 1, :] = squares_table
    reduce_copies = []
    for k in range(1, n_dp):
        target = lax.rem(me + k, n_dp)
        copy = pltpu.make_async_remote_copy(
            src_ref=table.at[target],
            dst_ref=sums_recv.at[k - 1],
            send_sem=sums_send_sem.at[k - 1],
            recv_sem=sums_recv_sem.at[k - 1],
            device_id={"dp": target},
            device_id_type=MESH,
        )
        copy.start()
        reduce_copies.append(copy)
    total = table[me]
    for k in range(1, n_dp):
        reduce_copies[k - 1].wait_recv()
        total = total + sums_recv[k - 1]
    count = images * positions
    mean_rows = total[0:1] / count
    variance = total[1:2] / count - mean_rows * mean_rows
    stats[0:1, :] = mean_rows
    stats[1:2, :] = lax.rsqrt(variance + epsilon) * gain_ref[...]
    gather_copies = []
    for k in range(1, n_dp):
        target = lax.rem(me + k, n_dp)
        copy = pltpu.make_async_remote_copy(
            src_ref=stats,
            dst_ref=stats_recv.at[k - 1],
            send_sem=stats_send_sem.at[k - 1],
            recv_sem=stats_recv_sem.at[k - 1],
            device_id={"dp": target},
            device_id_type=MESH,
        )
        copy.start()
        gather_copies.append(copy)

    image_row = lax.broadcasted_iota(jnp.int32, (images, channels), 0)
    dest_row = jnp.zeros((images, channels), jnp.int32)
    for i in range(images):
        dest_row = jnp.where(image_row == i, dests[i], dest_row)
    mean_image = jnp.zeros((images, channels), jnp.float32)
    scale_image = jnp.zeros((images, channels), jnp.float32)
    for k in range(n_dp):
        if k == 0:
            owner, ref = me, stats
        else:
            gather_copies[k - 1].wait_recv()
            owner, ref = lax.rem(me + n_dp - k, n_dp), stats_recv.at[k - 1]
        hit = dest_row == owner
        mean_image = jnp.where(hit, ref[0:1, :], mean_image)
        scale_image = jnp.where(hit, ref[1:2, :], scale_image)
    normed = (projected - mean_image[:, None, :]) * scale_image[:, None, :] + bias_ref[...][None]
    out_ref[...] = normed.astype(jnp.bfloat16).reshape(rows, channels)

    keys_peer.wait_send()
    for s in shared:
        shared[s].wait_send()
    for copy in pending + reduce_copies + gather_copies:
        copy.wait_send()


def local_fused(n_dp, keys, residual, se_reduce, se_expand, conv_weight, bn_gain, bn_bias, shuffle, unshuffle):
    images, positions, channels = keys.shape
    layers, rows_dev, _ = conv_weight.shape
    units = se_reduce.shape[1]
    rows = images * positions
    half = 2 * rows_dev
    window = -(-half // lane) * lane
    bf16, f32 = jnp.bfloat16, jnp.float32
    vmem = pl.BlockSpec(memory_space=pltpu.VMEM)
    anywhere = pl.BlockSpec(memory_space=pl.ANY)
    dma = pltpu.SemaphoreType.DMA
    normed = pl.pallas_call(
        functools.partial(fused_kernel, n_dp, images, positions),
        out_shape=jax.ShapeDtypeStruct((rows, channels), bf16),
        in_specs=[anywhere] * 4 + [vmem] * 2 + [pl.BlockSpec(memory_space=pltpu.SMEM)],
        out_specs=vmem,
        scratch_shapes=[
            pltpu.VMEM((layers, window, channels), bf16),
            pltpu.VMEM((window, units), bf16),
            pltpu.VMEM((window, units), bf16),
            pltpu.VMEM((2, rows, window), bf16),
            pltpu.VMEM((layers - 1, 2 * rows, window), bf16),
            pltpu.VMEM((layers - 1, 2 * rows, window), bf16),
            pltpu.VMEM((2 * images, units), f32),
            pltpu.VMEM((2 * images, units), f32),
            pltpu.VMEM((2, rows, window), bf16),
            pltpu.VMEM((rows, channels), bf16),
            pltpu.VMEM((rows, channels), bf16),
            pltpu.VMEM((n_dp, 2, channels), f32),
            pltpu.VMEM((n_dp - 1, 2, channels), f32),
            pltpu.VMEM((2, channels), f32),
            pltpu.VMEM((n_dp - 1, 2, channels), f32),
            dma((3,)),
            dma((3, layers + 2)),
            dma((layers - 1, 2)),
            dma((2,)),
            dma((2,)),
            dma((n_dp - 1,)),
            dma((n_dp - 1,)),
            dma((n_dp - 1,)),
            dma((n_dp - 1,)),
        ],
        compiler_params=pltpu.CompilerParams(collective_id=0, has_side_effects=True),
        name="fused_encoder",
    )(
        keys.reshape(rows, channels),
        se_reduce,
        se_expand,
        conv_weight,
        bn_gain.reshape(1, channels),
        bn_bias.reshape(1, channels),
        shuffle,
    )
    normed = normed.reshape(images, positions, channels)
    encoded = jax.nn.relu(normed.astype(f32) + residual.astype(f32))
    return encoded.astype(bf16)


def solution(mesh):
    placed = (
        P(("dp", "fsdp"), None, None),
        P(("dp", "fsdp"), None, None),
        P("fsdp", None),
        P("fsdp", None),
        P(None, "fsdp", None),
        P(),
        P(),
        P(("dp", "fsdp")),
        P(("dp", "fsdp")),
    )
    n_dp, n_fsdp = mesh.shape["dp"], mesh.shape["fsdp"]
    if n_fsdp == 4:
        local = functools.partial(local_fused, n_dp)
    else:
        local = local_general
    return jax.shard_map(
        local, mesh=mesh, in_specs=placed, out_specs=P(("dp", "fsdp"), None, None), check_vma=False
    )
```

```python
import functools

import jax
import jax.numpy as jnp
from jax import lax
from jax.experimental import pallas as pl
from jax.experimental.pallas import tpu as pltpu
from jax.sharding import PartitionSpec as P

epsilon = 1e-05
lane = 128
MESH = pl.DeviceIdType.MESH


def project_rows(flat, weight_rows):
    return jnp.dot(
        flat,
        lax.all_gather(weight_rows, "fsdp", axis=0, tiled=True),
        preferred_element_type=jnp.float32,
    )


def encode_block(batch_block, reduce_full, expand_full, conv_weight):
    images, positions, channels = batch_block.shape
    layers = conv_weight.shape[0]
    flat = batch_block.reshape(images * positions, channels)
    for layer in range(layers - 1):
        flat = jax.nn.relu(project_rows(flat, conv_weight[layer])).astype(jnp.bfloat16)
    entry = flat.reshape(images, positions, channels)
    pooled = jnp.mean(entry, axis=1, dtype=jnp.float32).astype(jnp.bfloat16)
    squeeze_act = jax.nn.relu(
        jnp.dot(pooled, reduce_full, preferred_element_type=jnp.float32)
    ).astype(jnp.bfloat16)
    excite = jax.nn.sigmoid(
        lax.dot_general(
            squeeze_act, expand_full, (((1,), (1,)), ((), ())), preferred_element_type=jnp.float32
        )
    )
    scaled = (entry * excite[:, None, :]).astype(jnp.bfloat16).reshape(images * positions, channels)
    projected = project_rows(scaled, conv_weight[layers - 1])
    return projected.reshape(images, positions, channels)


def local_general(keys, residual, se_reduce, se_expand, conv_weight, bn_gain, bn_bias, shuffle, unshuffle):
    images, positions, channels = keys.shape
    count = images * positions
    reduce_full, expand_full = (
        lax.all_gather(se_reduce, "fsdp", axis=0, tiled=True),
        lax.all_gather(se_expand, "fsdp", axis=0, tiled=True),
    )
    send_order = jnp.argsort(shuffle)
    back_order = jnp.argsort(send_order)
    outgoing = jnp.take(keys, send_order, axis=0)
    arrived = lax.all_to_all(outgoing, "dp", split_axis=0, concat_axis=0, tiled=True)
    projected = encode_block(arrived, reduce_full, expand_full, conv_weight)
    row_sums = jnp.sum(projected, axis=(0, 1))
    square_sums = jnp.sum(projected * projected, axis=(0, 1))
    mean_rows = row_sums / count
    variance = square_sums / count - mean_rows * mean_rows
    scale_rows = lax.rsqrt(variance + epsilon) * bn_gain
    normed_here = ((projected - mean_rows) * scale_rows + bn_bias).astype(jnp.bfloat16)
    returned = lax.all_to_all(normed_here, "dp", split_axis=0, concat_axis=0, tiled=True)
    normed = jnp.take(returned, back_order, axis=0)
    encoded = jax.nn.relu(normed.astype(jnp.float32) + residual.astype(jnp.float32))
    return encoded.astype(jnp.bfloat16)


def fused_kernel(
    n_dp,
    images,
    positions,
    keys_ref,
    reduce_ref,
    expand_ref,
    weight_ref,
    gain_ref,
    bias_ref,
    shuffle_ref,
    out_ref,
    w,
    red,
    exp,
    kbuf,
    psend,
    precv,
    se_send,
    se_recv,
    last_send,
    last_recv,
    table,
    sums_recv,
    stats,
    stats_recv,
    key_sem,
    weight_sem,
    layer_sem,
    se_sem,
    last_sem,
    sums_send_sem,
    sums_recv_sem,
    stats_send_sem,
    stats_recv_sem,
    ready_sem,
):
    me = lax.axis_index("dp")
    f = lax.axis_index("fsdp")
    x, c = f // 2, f % 2
    sibling = 2 * x + (1 - c)
    peer = 2 * (1 - x) + c
    layers, rows_dev, channels = weight_ref.shape
    half = 2 * rows_dev
    window = kbuf.shape[2]
    pad = window - half
    rows = images * positions
    own_lo = pl.multiple_of(x * (channels - window), lane)
    peer_lo = pl.multiple_of((1 - x) * (channels - window), lane)
    base = pl.multiple_of(x * pad + c * rows_dev, 16)

    keys_own = pltpu.make_async_copy(
        keys_ref.at[:, pl.ds(own_lo, window)], kbuf.at[x], key_sem.at[0]
    )
    keys_own.start()
    sources = [weight_ref.at[l] for l in range(layers)] + [reduce_ref, expand_ref]
    targets = [w.at[l] for l in range(layers)] + [red, exp]
    local_copies = []
    for s, (src, dst) in enumerate(zip(sources, targets)):
        copy = pltpu.make_async_copy(src, dst.at[pl.ds(base, rows_dev), :], weight_sem.at[0, s])
        copy.start()
        local_copies.append(copy)

    zero_lo = pl.multiple_of((1 - x) * half, 16)
    for l in range(layers):
        w[l, pl.ds(zero_lo, pad), :] = jnp.zeros((pad, channels), w.dtype)
    red[pl.ds(zero_lo, pad), :] = jnp.zeros((pad, red.shape[1]), red.dtype)
    exp[pl.ds(zero_lo, pad), :] = jnp.zeros((pad, exp.shape[1]), exp.dtype)

    barrier = pltpu.get_barrier_semaphore()
    pl.semaphore_signal(barrier, inc=1, device_id={"fsdp": peer}, device_id_type=MESH)
    for k in range(1, n_dp):
        pl.semaphore_signal(
            barrier, inc=1, device_id={"dp": lax.rem(me + k, n_dp)}, device_id_type=MESH
        )

    @pl.when(c == 0)
    def _():
        pl.semaphore_signal(barrier, inc=1, device_id={"fsdp": sibling}, device_id_type=MESH)

    pl.semaphore_wait(barrier, n_dp + c)

    @pl.when(c == 1)
    def _():
        pl.semaphore_signal(ready_sem, inc=1, device_id={"fsdp": sibling}, device_id_type=MESH)

    keys_peer = pltpu.make_async_remote_copy(
        src_ref=keys_ref.at[:, pl.ds(peer_lo, window)],
        dst_ref=kbuf.at[x],
        send_sem=key_sem.at[1],
        recv_sem=key_sem.at[2],
        device_id={"fsdp": peer},
        device_id_type=MESH,
    )
    keys_peer.start()

    @pl.when(c == 0)
    def _():
        pl.semaphore_wait(ready_sem, 1)

    shared = {}
    for s in (0, 1, layers, layers + 1, *range(2, layers)):
        shared[s] = pltpu.make_async_remote_copy(
            src_ref=sources[s],
            dst_ref=targets[s].at[pl.ds(base, rows_dev), :],
            send_sem=weight_sem.at[1, s],
            recv_sem=weight_sem.at[2, s],
            device_id={"fsdp": sibling},
            device_id_type=MESH,
        )
        shared[s].start()

    def have_weights(s):
        local_copies[s].wait()
        shared[s].wait_recv()

    pending = []

    def to_peer(src, dst, sems):
        copy = pltpu.make_async_remote_copy(
            src_ref=src,
            dst_ref=dst,
            send_sem=sems.at[0],
            recv_sem=sems.at[1],
            device_id={"fsdp": peer},
            device_id_type=MESH,
        )
        copy.start()
        pending.append(copy)
        return copy

    chunks = psend.shape[1]
    part_rows = rows // chunks
    part_images = 2 * images // chunks
    keys_own.wait()
    keys_peer.wait_recv()
    entries = [
        kbuf[:, j * part_rows : (j + 1) * part_rows, :].reshape(2 * part_rows, window)
        for j in range(chunks)
    ]
    copies = [None] * chunks
    mines = [None] * chunks

    def settle(l, j):
        copies[j].wait_recv()
        full = mines[j] + precv[l, j].astype(jnp.float32)
        return jnp.maximum(full, 0.0).astype(jnp.bfloat16)

    for l in range(layers - 1):
        have_weights(l)
        for j in range(chunks):
            if l > 0:
                entries[j] = settle(l - 1, j)
            theirs = jnp.dot(
                entries[j], w[l, :, pl.ds(peer_lo, window)], preferred_element_type=jnp.float32
            )
            psend[l, j] = theirs.astype(jnp.bfloat16)
            copies[j] = to_peer(psend.at[l, j], precv.at[l, j], layer_sem.at[l, j])
            mines[j] = jnp.dot(
                entries[j], w[l, :, pl.ds(own_lo, window)], preferred_element_type=jnp.float32
            )

    have_weights(layers)
    have_weights(layers + 1)
    wides, parts = [None] * chunks, [None] * chunks
    for j in range(chunks):
        entry = settle(layers - 2, j)
        wides[j] = entry.astype(jnp.float32).reshape(part_images, positions, window)
        pooled = (jnp.sum(wides[j], axis=1) * (1.0 / positions)).astype(jnp.bfloat16)
        parts[j] = jnp.dot(pooled, red[...], preferred_element_type=jnp.float32)
        se_send[j] = parts[j]
        copies[j] = to_peer(se_send.at[j], se_recv.at[j], se_sem.at[j])

    have_weights(layers - 1)
    for j in range(chunks):
        copies[j].wait_recv()
        squeeze_act = jnp.maximum(parts[j] + se_recv[j], 0.0).astype(jnp.bfloat16)
        excite = jax.nn.sigmoid(
            lax.dot_general(
                squeeze_act, exp[...], (((1,), (1,)), ((), ())), preferred_element_type=jnp.float32
            )
        )
        scaled = (wides[j] * excite[:, None, :]).astype(jnp.bfloat16)
        both = jnp.dot(
            scaled.reshape(2 * part_rows, window), w[layers - 1], preferred_element_type=jnp.float32
        )
        low, high = both[:part_rows], both[part_rows:]
        last_send[j] = jnp.where(x == 0, high, low).astype(jnp.bfloat16)
        copies[j] = to_peer(last_send.at[j], last_recv.at[j], last_sem.at[j])
        mines[j] = jnp.where(x == 0, low, high)
    for j in range(chunks):
        copies[j].wait_recv()
        mines[j] = mines[j] + last_recv[j].astype(jnp.float32)
    projected = jnp.concatenate(mines, axis=0).reshape(images, positions, channels)

    image_sums = jnp.sum(projected, axis=1)
    image_squares = jnp.sum(projected * projected, axis=1)
    dests = [lax.div(shuffle_ref[i], images) for i in range(images)]
    device_row = lax.broadcasted_iota(jnp.int32, (n_dp, channels), 0)
    sums_table = jnp.zeros((n_dp, channels), jnp.float32)
    squares_table = jnp.zeros((n_dp, channels), jnp.float32)
    for i in range(images):
        hit = device_row == dests[i]
        sums_table = sums_table + jnp.where(hit, image_sums[i : i + 1], 0.0)
        squares_table = squares_table + jnp.where(hit, image_squares[i : i + 1], 0.0)
    table[:, 0, :] = sums_table
    table[:, 1, :] = squares_table
    reduce_copies = []
    for k in range(1, n_dp):
        target = lax.rem(me + k, n_dp)
        copy = pltpu.make_async_remote_copy(
            src_ref=table.at[target],
            dst_ref=sums_recv.at[k - 1],
            send_sem=sums_send_sem.at[k - 1],
            recv_sem=sums_recv_sem.at[k - 1],
            device_id={"dp": target},
            device_id_type=MESH,
        )
        copy.start()
        reduce_copies.append(copy)
    total = table[me]
    for k in range(1, n_dp):
        reduce_copies[k - 1].wait_recv()
        total = total + sums_recv[k - 1]
    count = images * positions
    mean_rows = total[0:1] / count
    variance = total[1:2] / count - mean_rows * mean_rows
    stats[0:1, :] = mean_rows
    stats[1:2, :] = lax.rsqrt(variance + epsilon) * gain_ref[...].reshape(1, channels)
    gather_copies = []
    for k in range(1, n_dp):
        target = lax.rem(me + k, n_dp)
        copy = pltpu.make_async_remote_copy(
            src_ref=stats,
            dst_ref=stats_recv.at[k - 1],
            send_sem=stats_send_sem.at[k - 1],
            recv_sem=stats_recv_sem.at[k - 1],
            device_id={"dp": target},
            device_id_type=MESH,
        )
        copy.start()
        gather_copies.append(copy)

    image_row = lax.broadcasted_iota(jnp.int32, (images, channels), 0)
    dest_row = jnp.zeros((images, channels), jnp.int32)
    for i in range(images):
        dest_row = jnp.where(image_row == i, dests[i], dest_row)
    mean_image = jnp.zeros((images, channels), jnp.float32)
    scale_image = jnp.zeros((images, channels), jnp.float32)
    for k in range(n_dp):
        if k == 0:
            owner, ref = me, stats
        else:
            gather_copies[k - 1].wait_recv()
            owner, ref = lax.rem(me + n_dp - k, n_dp), stats_recv.at[k - 1]
        hit = dest_row == owner
        mean_image = jnp.where(hit, ref[0:1, :], mean_image)
        scale_image = jnp.where(hit, ref[1:2, :], scale_image)
    normed = (projected - mean_image[:, None, :]) * scale_image[:, None, :] + bias_ref[...].reshape(1, 1, channels)
    out_ref[...] = normed.astype(jnp.bfloat16).reshape(rows, channels)

    keys_peer.wait_send()
    for s in shared:
        shared[s].wait_send()
    for copy in pending + reduce_copies + gather_copies:
        copy.wait_send()


def local_fused(n_dp, keys, residual, se_reduce, se_expand, conv_weight, bn_gain, bn_bias, shuffle, unshuffle):
    images, positions, channels = keys.shape
    layers, rows_dev, _ = conv_weight.shape
    units = se_reduce.shape[1]
    chunks = 2
    rows = images * positions
    half = 2 * rows_dev
    window = -(-half // lane) * lane
    bf16, f32 = jnp.bfloat16, jnp.float32
    vmem = pl.BlockSpec(memory_space=pltpu.VMEM)
    anywhere = pl.BlockSpec(memory_space=pl.ANY)
    dma = pltpu.SemaphoreType.DMA
    normed = pl.pallas_call(
        functools.partial(fused_kernel, n_dp, images, positions),
        out_shape=jax.ShapeDtypeStruct((rows, channels), bf16),
        in_specs=[anywhere] * 4 + [vmem] * 2 + [pl.BlockSpec(memory_space=pltpu.SMEM)],
        out_specs=vmem,
        scratch_shapes=[
            pltpu.VMEM((layers, window, channels), bf16),
            pltpu.VMEM((window, units), bf16),
            pltpu.VMEM((window, units), bf16),
            pltpu.VMEM((2, rows, window), bf16),
            pltpu.VMEM((layers - 1, chunks, 2 * rows // chunks, window), bf16),
            pltpu.VMEM((layers - 1, chunks, 2 * rows // chunks, window), bf16),
            pltpu.VMEM((chunks, 2 * images // chunks, units), f32),
            pltpu.VMEM((chunks, 2 * images // chunks, units), f32),
            pltpu.VMEM((chunks, rows // chunks, channels), bf16),
            pltpu.VMEM((chunks, rows // chunks, channels), bf16),
            pltpu.VMEM((n_dp, 2, channels), f32),
            pltpu.VMEM((n_dp - 1, 2, channels), f32),
            pltpu.VMEM((2, channels), f32),
            pltpu.VMEM((n_dp - 1, 2, channels), f32),
            dma((3,)),
            dma((3, layers + 2)),
            dma((layers - 1, chunks, 2)),
            dma((chunks, 2)),
            dma((chunks, 2)),
            dma((n_dp - 1,)),
            dma((n_dp - 1,)),
            dma((n_dp - 1,)),
            dma((n_dp - 1,)),
            pltpu.SemaphoreType.REGULAR,
        ],
        compiler_params=pltpu.CompilerParams(collective_id=0, has_side_effects=True),
        name="fused_encoder",
    )(
        keys.reshape(rows, channels),
        se_reduce,
        se_expand,
        conv_weight,
        bn_gain,
        bn_bias,
        shuffle,
    )
    normed = normed.reshape(images, positions, channels)
    encoded = jax.nn.relu(normed.astype(f32) + residual.astype(f32))
    return encoded.astype(bf16)


def solution(mesh):
    placed = (
        P(("dp", "fsdp"), None, None),
        P(("dp", "fsdp"), None, None),
        P("fsdp", None),
        P("fsdp", None),
        P(None, "fsdp", None),
        P(),
        P(),
        P(("dp", "fsdp")),
        P(("dp", "fsdp")),
    )
    n_dp, n_fsdp = mesh.shape["dp"], mesh.shape["fsdp"]
    if n_fsdp == 4:
        local = functools.partial(local_fused, n_dp)
    else:
        local = local_general
    return jax.shard_map(
        local, mesh=mesh, in_specs=placed, out_specs=P(("dp", "fsdp"), None, None), check_vma=False
    )
```

```python
import functools

import jax
import jax.numpy as jnp
from jax import lax
from jax.experimental import pallas as pl
from jax.experimental.pallas import tpu as pltpu
from jax.sharding import PartitionSpec as P

epsilon = 1e-05
lane = 128
MESH = pl.DeviceIdType.MESH


def project_rows(flat, weight_rows):
    return jnp.dot(
        flat,
        lax.all_gather(weight_rows, "fsdp", axis=0, tiled=True),
        preferred_element_type=jnp.float32,
    )


def encode_block(batch_block, reduce_full, expand_full, conv_weight):
    images, positions, channels = batch_block.shape
    layers = conv_weight.shape[0]
    flat = batch_block.reshape(images * positions, channels)
    for layer in range(layers - 1):
        flat = jax.nn.relu(project_rows(flat, conv_weight[layer])).astype(jnp.bfloat16)
    entry = flat.reshape(images, positions, channels)
    pooled = jnp.mean(entry, axis=1, dtype=jnp.float32).astype(jnp.bfloat16)
    squeeze_act = jax.nn.relu(
        jnp.dot(pooled, reduce_full, preferred_element_type=jnp.float32)
    ).astype(jnp.bfloat16)
    excite = jax.nn.sigmoid(
        lax.dot_general(
            squeeze_act, expand_full, (((1,), (1,)), ((), ())), preferred_element_type=jnp.float32
        )
    )
    scaled = (entry * excite[:, None, :]).astype(jnp.bfloat16).reshape(images * positions, channels)
    projected = project_rows(scaled, conv_weight[layers - 1])
    return projected.reshape(images, positions, channels)


def local_general(keys, residual, se_reduce, se_expand, conv_weight, bn_gain, bn_bias, shuffle, unshuffle):
    images, positions, channels = keys.shape
    count = images * positions
    reduce_full, expand_full = (
        lax.all_gather(se_reduce, "fsdp", axis=0, tiled=True),
        lax.all_gather(se_expand, "fsdp", axis=0, tiled=True),
    )
    send_order = jnp.argsort(shuffle)
    back_order = jnp.argsort(send_order)
    outgoing = jnp.take(keys, send_order, axis=0)
    arrived = lax.all_to_all(outgoing, "dp", split_axis=0, concat_axis=0, tiled=True)
    projected = encode_block(arrived, reduce_full, expand_full, conv_weight)
    row_sums = jnp.sum(projected, axis=(0, 1))
    square_sums = jnp.sum(projected * projected, axis=(0, 1))
    mean_rows = row_sums / count
    variance = square_sums / count - mean_rows * mean_rows
    scale_rows = lax.rsqrt(variance + epsilon) * bn_gain
    normed_here = ((projected - mean_rows) * scale_rows + bn_bias).astype(jnp.bfloat16)
    returned = lax.all_to_all(normed_here, "dp", split_axis=0, concat_axis=0, tiled=True)
    normed = jnp.take(returned, back_order, axis=0)
    encoded = jax.nn.relu(normed.astype(jnp.float32) + residual.astype(jnp.float32))
    return encoded.astype(jnp.bfloat16)


def fused_kernel(
    n_dp,
    images,
    positions,
    keys_ref,
    reduce_ref,
    expand_ref,
    weight_ref,
    gain_ref,
    bias_ref,
    shuffle_ref,
    out_ref,
    w,
    red,
    exp,
    kbuf,
    psend,
    precv,
    se_send,
    se_recv,
    last_send,
    last_recv,
    keysv,
    ksend,
    nsend,
    nrecv,
    key_sem,
    key_send_sem,
    key_recv_sem,
    weight_sem,
    layer_sem,
    se_sem,
    last_sem,
    back_send_sem,
    back_recv_sem,
    ready_sem,
):
    me = lax.axis_index("dp")
    f = lax.axis_index("fsdp")
    x, c = f // 2, f % 2
    sibling = 2 * x + (1 - c)
    peer = 2 * (1 - x) + c
    layers, rows_dev, channels = weight_ref.shape
    half = 2 * rows_dev
    window = kbuf.shape[3]
    pad = window - half
    rows = images * positions
    own_lo = pl.multiple_of(x * (channels - window), lane)
    peer_lo = pl.multiple_of((1 - x) * (channels - window), lane)
    base = pl.multiple_of(x * pad + c * rows_dev, 16)

    keys_local = pltpu.make_async_copy(keys_ref, keysv, key_sem)
    keys_local.start()
    sources = [weight_ref.at[l] for l in range(layers)] + [reduce_ref, expand_ref]
    targets = [w.at[l] for l in range(layers)] + [red, exp]
    local_copies = []
    for s, (src, dst) in enumerate(zip(sources, targets)):
        copy = pltpu.make_async_copy(src, dst.at[pl.ds(base, rows_dev), :], weight_sem.at[0, s])
        copy.start()
        local_copies.append(copy)

    zero_lo = pl.multiple_of((1 - x) * half, 16)
    for l in range(layers):
        w[l, pl.ds(zero_lo, pad), :] = jnp.zeros((pad, channels), w.dtype)
    red[pl.ds(zero_lo, pad), :] = jnp.zeros((pad, red.shape[1]), red.dtype)
    exp[pl.ds(zero_lo, pad), :] = jnp.zeros((pad, exp.shape[1]), exp.dtype)

    dests = [lax.div(shuffle_ref[i], images) for i in range(images)]
    keys_local.wait()
    for e in range(n_dp):
        chosen = jnp.int32(0)
        for i in range(images):
            chosen = jnp.where(dests[i] == e, i, chosen)
        ksend[e] = keysv[chosen]

    barrier = pltpu.get_barrier_semaphore()
    for k in range(n_dp):
        target = lax.rem(me + k, n_dp)
        for column in (f, peer):
            if k > 0 or column is peer:
                pl.semaphore_signal(
                    barrier,
                    inc=1,
                    device_id={"dp": target, "fsdp": column},
                    device_id_type=MESH,
                )

    @pl.when(c == 0)
    def _():
        pl.semaphore_signal(barrier, inc=1, device_id={"fsdp": sibling}, device_id_type=MESH)

    pl.semaphore_wait(barrier, 2 * n_dp - 1 + c)

    @pl.when(c == 1)
    def _():
        pl.semaphore_signal(ready_sem, inc=1, device_id={"fsdp": sibling}, device_id_type=MESH)

    key_copies = []
    for k in range(n_dp):
        target = lax.rem(me + k, n_dp)
        for side, (column, lo) in enumerate(((f, own_lo), (peer, peer_lo))):
            src = ksend.at[target, :, pl.ds(lo, window)]
            dst = kbuf.at[x, me]
            if k == 0 and side == 0:
                copy = pltpu.make_async_copy(src, dst, key_recv_sem.at[side, k])
            else:
                copy = pltpu.make_async_remote_copy(
                    src_ref=src,
                    dst_ref=dst,
                    send_sem=key_send_sem.at[side, k],
                    recv_sem=key_recv_sem.at[side, k],
                    device_id={"dp": target, "fsdp": column},
                    device_id_type=MESH,
                )
            copy.start()
            key_copies.append(copy)

    @pl.when(c == 0)
    def _():
        pl.semaphore_wait(ready_sem, 1)

    shared = {}
    for s in (0, 1, layers, layers + 1, *range(2, layers)):
        shared[s] = pltpu.make_async_remote_copy(
            src_ref=sources[s],
            dst_ref=targets[s].at[pl.ds(base, rows_dev), :],
            send_sem=weight_sem.at[1, s],
            recv_sem=weight_sem.at[2, s],
            device_id={"fsdp": sibling},
            device_id_type=MESH,
        )
        shared[s].start()

    def have_weights(s):
        local_copies[s].wait()
        shared[s].wait_recv()

    pending = []

    def to_peer(src, dst, sems):
        copy = pltpu.make_async_remote_copy(
            src_ref=src,
            dst_ref=dst,
            send_sem=sems.at[0],
            recv_sem=sems.at[1],
            device_id={"fsdp": peer},
            device_id_type=MESH,
        )
        copy.start()
        pending.append(copy)
        return copy

    chunks = psend.shape[1]
    part_rows = rows // chunks
    part_images = 2 * images // chunks
    key_copies[0].wait()
    for copy in key_copies[1:]:
        copy.wait_recv()
    half_images = images // chunks
    entries = [
        kbuf[:, j * half_images : (j + 1) * half_images]
        .astype(jnp.float32)
        .reshape(2 * part_rows, window)
        .astype(jnp.bfloat16)
        for j in range(chunks)
    ]
    copies = [None] * chunks
    mines = [None] * chunks

    def settle(l, j):
        copies[j].wait_recv()
        full = mines[j] + precv[l, j].astype(jnp.float32)
        return jnp.maximum(full, 0.0).astype(jnp.bfloat16)

    for l in range(layers - 1):
        have_weights(l)
        for j in range(chunks):
            if l > 0:
                entries[j] = settle(l - 1, j)
            theirs = jnp.dot(
                entries[j], w[l, :, pl.ds(peer_lo, window)], preferred_element_type=jnp.float32
            )
            psend[l, j] = theirs.astype(jnp.bfloat16)
            copies[j] = to_peer(psend.at[l, j], precv.at[l, j], layer_sem.at[l, j])
            mines[j] = jnp.dot(
                entries[j], w[l, :, pl.ds(own_lo, window)], preferred_element_type=jnp.float32
            )

    have_weights(layers)
    have_weights(layers + 1)
    wides, parts = [None] * chunks, [None] * chunks
    for j in range(chunks):
        entry = settle(layers - 2, j)
        wides[j] = entry.astype(jnp.float32).reshape(part_images, positions, window)
        pooled = (jnp.sum(wides[j], axis=1) * (1.0 / positions)).astype(jnp.bfloat16)
        parts[j] = jnp.dot(pooled, red[...], preferred_element_type=jnp.float32)
        se_send[j] = parts[j]
        copies[j] = to_peer(se_send.at[j], se_recv.at[j], se_sem.at[j])

    have_weights(layers - 1)
    for j in range(chunks):
        copies[j].wait_recv()
        squeeze_act = jnp.maximum(parts[j] + se_recv[j], 0.0).astype(jnp.bfloat16)
        excite = jax.nn.sigmoid(
            lax.dot_general(
                squeeze_act, exp[...], (((1,), (1,)), ((), ())), preferred_element_type=jnp.float32
            )
        )
        scaled = (wides[j] * excite[:, None, :]).astype(jnp.bfloat16)
        both = jnp.dot(
            scaled.reshape(2 * part_rows, window), w[layers - 1], preferred_element_type=jnp.float32
        )
        low, high = both[:part_rows], both[part_rows:]
        last_send[j] = jnp.where(x == 0, high, low).astype(jnp.bfloat16)
        copies[j] = to_peer(last_send.at[j], last_recv.at[j], last_sem.at[j])
        mines[j] = jnp.where(x == 0, low, high)
    for j in range(chunks):
        copies[j].wait_recv()
        mines[j] = mines[j] + last_recv[j].astype(jnp.float32)
    count = images * positions
    mean_rows = sum(jnp.sum(mine, axis=0, keepdims=True) for mine in mines) / count
    squares = sum(jnp.sum(mine * mine, axis=0, keepdims=True) for mine in mines) / count
    scale_rows = lax.rsqrt(squares - mean_rows * mean_rows + epsilon) * gain_ref[...].reshape(
        1, channels
    )
    bias_rows = bias_ref[...].reshape(1, channels)
    for j in range(chunks):
        normed = (mines[j] - mean_rows) * scale_rows + bias_rows
        nsend[j * half_images : (j + 1) * half_images] = normed.reshape(
            half_images, positions, channels
        ).astype(jnp.bfloat16)

    back_copies = []
    for k in range(1, n_dp):
        target = lax.rem(me + k, n_dp)
        copy = pltpu.make_async_remote_copy(
            src_ref=nsend.at[target],
            dst_ref=nrecv.at[me],
            send_sem=back_send_sem.at[k - 1],
            recv_sem=back_recv_sem.at[k - 1],
            device_id={"dp": target},
            device_id_type=MESH,
        )
        copy.start()
        back_copies.append(copy)
    nrecv[me] = nsend[me]
    for copy in key_copies[1:] + list(shared.values()) + pending:
        copy.wait_send()
    for copy in back_copies:
        copy.wait_recv()
    for i in range(images):
        out_ref[i] = nrecv[dests[i]]
    for copy in back_copies:
        copy.wait_send()


def local_fused(n_dp, keys, residual, se_reduce, se_expand, conv_weight, bn_gain, bn_bias, shuffle, unshuffle):
    images, positions, channels = keys.shape
    layers, rows_dev, _ = conv_weight.shape
    units = se_reduce.shape[1]
    chunks = 2
    rows = images * positions
    half = 2 * rows_dev
    window = -(-half // lane) * lane
    bf16, f32 = jnp.bfloat16, jnp.float32
    vmem = pl.BlockSpec(memory_space=pltpu.VMEM)
    anywhere = pl.BlockSpec(memory_space=pl.ANY)
    dma = pltpu.SemaphoreType.DMA
    normed = pl.pallas_call(
        functools.partial(fused_kernel, n_dp, images, positions),
        out_shape=jax.ShapeDtypeStruct((images, positions, channels), bf16),
        in_specs=[anywhere] * 4 + [vmem] * 2 + [pl.BlockSpec(memory_space=pltpu.SMEM)],
        out_specs=vmem,
        scratch_shapes=[
            pltpu.VMEM((layers, window, channels), bf16),
            pltpu.VMEM((window, units), bf16),
            pltpu.VMEM((window, units), bf16),
            pltpu.VMEM((2, images, positions, window), bf16),
            pltpu.VMEM((layers - 1, chunks, 2 * rows // chunks, window), bf16),
            pltpu.VMEM((layers - 1, chunks, 2 * rows // chunks, window), bf16),
            pltpu.VMEM((chunks, 2 * images // chunks, units), f32),
            pltpu.VMEM((chunks, 2 * images // chunks, units), f32),
            pltpu.VMEM((chunks, rows // chunks, channels), bf16),
            pltpu.VMEM((chunks, rows // chunks, channels), bf16),
            pltpu.VMEM((images, positions, channels), bf16),
            pltpu.VMEM((n_dp, positions, channels), bf16),
            pltpu.VMEM((images, positions, channels), bf16),
            pltpu.VMEM((n_dp, positions, channels), bf16),
            dma,
            dma((2, n_dp)),
            dma((2, n_dp)),
            dma((3, layers + 2)),
            dma((layers - 1, chunks, 2)),
            dma((chunks, 2)),
            dma((chunks, 2)),
            dma((n_dp - 1,)),
            dma((n_dp - 1,)),
            pltpu.SemaphoreType.REGULAR,
        ],
        compiler_params=pltpu.CompilerParams(collective_id=0, has_side_effects=True),
        name="fused_encoder",
    )(
        keys,
        se_reduce,
        se_expand,
        conv_weight,
        bn_gain,
        bn_bias,
        shuffle,
    )
    encoded = jax.nn.relu(normed.astype(f32) + residual.astype(f32))
    return encoded.astype(bf16)


def solution(mesh):
    placed = (
        P(("dp", "fsdp"), None, None),
        P(("dp", "fsdp"), None, None),
        P("fsdp", None),
        P("fsdp", None),
        P(None, "fsdp", None),
        P(),
        P(),
        P(("dp", "fsdp")),
        P(("dp", "fsdp")),
    )
    n_dp, n_fsdp = mesh.shape["dp"], mesh.shape["fsdp"]

    def local(keys, *others):
        if n_fsdp == 4 and keys.shape[0] == n_dp:
            return local_fused(n_dp, keys, *others)
        return local_general(keys, *others)

    return jax.shard_map(
        local, mesh=mesh, in_specs=placed, out_specs=P(("dp", "fsdp"), None, None), check_vma=False
    )
```

```python
import functools

import jax
import jax.numpy as jnp
from jax import lax
from jax.experimental import pallas as pl
from jax.experimental.pallas import tpu as pltpu
from jax.sharding import PartitionSpec as P

epsilon = 1e-05
lane = 128
MESH = pl.DeviceIdType.MESH


def project_rows(flat, weight_rows):
    return jnp.dot(
        flat,
        lax.all_gather(weight_rows, "fsdp", axis=0, tiled=True),
        preferred_element_type=jnp.float32,
    )


def encode_block(batch_block, reduce_full, expand_full, conv_weight):
    images, positions, channels = batch_block.shape
    layers = conv_weight.shape[0]
    flat = batch_block.reshape(images * positions, channels)
    for layer in range(layers - 1):
        flat = jax.nn.relu(project_rows(flat, conv_weight[layer])).astype(jnp.bfloat16)
    entry = flat.reshape(images, positions, channels)
    pooled = jnp.mean(entry, axis=1, dtype=jnp.float32).astype(jnp.bfloat16)
    squeeze_act = jax.nn.relu(
        jnp.dot(pooled, reduce_full, preferred_element_type=jnp.float32)
    ).astype(jnp.bfloat16)
    excite = jax.nn.sigmoid(
        lax.dot_general(
            squeeze_act, expand_full, (((1,), (1,)), ((), ())), preferred_element_type=jnp.float32
        )
    )
    scaled = (entry * excite[:, None, :]).astype(jnp.bfloat16).reshape(images * positions, channels)
    projected = project_rows(scaled, conv_weight[layers - 1])
    return projected.reshape(images, positions, channels)


def local_general(keys, residual, se_reduce, se_expand, conv_weight, bn_gain, bn_bias, shuffle, unshuffle):
    images, positions, channels = keys.shape
    count = images * positions
    reduce_full, expand_full = (
        lax.all_gather(se_reduce, "fsdp", axis=0, tiled=True),
        lax.all_gather(se_expand, "fsdp", axis=0, tiled=True),
    )
    send_order = jnp.argsort(shuffle)
    back_order = jnp.argsort(send_order)
    outgoing = jnp.take(keys, send_order, axis=0)
    arrived = lax.all_to_all(outgoing, "dp", split_axis=0, concat_axis=0, tiled=True)
    projected = encode_block(arrived, reduce_full, expand_full, conv_weight)
    row_sums = jnp.sum(projected, axis=(0, 1))
    square_sums = jnp.sum(projected * projected, axis=(0, 1))
    mean_rows = row_sums / count
    variance = square_sums / count - mean_rows * mean_rows
    scale_rows = lax.rsqrt(variance + epsilon) * bn_gain
    normed_here = ((projected - mean_rows) * scale_rows + bn_bias).astype(jnp.bfloat16)
    returned = lax.all_to_all(normed_here, "dp", split_axis=0, concat_axis=0, tiled=True)
    normed = jnp.take(returned, back_order, axis=0)
    encoded = jax.nn.relu(normed.astype(jnp.float32) + residual.astype(jnp.float32))
    return encoded.astype(jnp.bfloat16)


def fused_kernel(
    n_dp,
    images,
    positions,
    keys_ref,
    reduce_ref,
    expand_ref,
    weight_ref,
    gain_ref,
    bias_ref,
    shuffle_ref,
    out_ref,
    w,
    red,
    exp,
    kbuf,
    psend,
    precv,
    se_send,
    se_recv,
    last_send,
    last_recv,
    keysv,
    ksend,
    nsend,
    nrecv,
    key_sem,
    key_send_sem,
    key_recv_sem,
    weight_sem,
    layer_sem,
    se_sem,
    last_sem,
    back_send_sem,
    back_recv_sem,
    ready_sem,
):
    me = lax.axis_index("dp")
    f = lax.axis_index("fsdp")
    x, c = f // 2, f % 2
    sibling = 2 * x + (1 - c)
    peer = 2 * (1 - x) + c
    layers, rows_dev, channels = weight_ref.shape
    half = 2 * rows_dev
    window = kbuf.shape[3]
    pad = window - half
    rows = images * positions
    own_lo = pl.multiple_of(x * (channels - window), lane)
    peer_lo = pl.multiple_of((1 - x) * (channels - window), lane)
    base = pl.multiple_of(x * pad + c * rows_dev, 16)

    keys_local = pltpu.make_async_copy(keys_ref, keysv, key_sem)
    keys_local.start()
    sources = [weight_ref.at[l] for l in range(layers)] + [reduce_ref, expand_ref]
    targets = [w.at[l] for l in range(layers)] + [red, exp]
    local_copies = []
    for s, (src, dst) in enumerate(zip(sources, targets)):
        copy = pltpu.make_async_copy(src, dst.at[pl.ds(base, rows_dev), :], weight_sem.at[0, s])
        copy.start()
        local_copies.append(copy)

    zero_lo = pl.multiple_of((1 - x) * half, 16)
    for l in range(layers):
        w[l, pl.ds(zero_lo, pad), :] = jnp.zeros((pad, channels), w.dtype)
    red[pl.ds(zero_lo, pad), :] = jnp.zeros((pad, red.shape[1]), red.dtype)
    exp[pl.ds(zero_lo, pad), :] = jnp.zeros((pad, exp.shape[1]), exp.dtype)

    dests = [lax.div(shuffle_ref[i], images) for i in range(images)]
    keys_local.wait()
    for e in range(n_dp):
        chosen = jnp.int32(0)
        for i in range(images):
            chosen = jnp.where(dests[i] == e, i, chosen)
        ksend[e] = keysv[chosen]

    barrier = pltpu.get_barrier_semaphore()
    for k in range(n_dp):
        target = lax.rem(me + k, n_dp)
        for column in (f, peer):
            if k > 0 or column is peer:
                pl.semaphore_signal(
                    barrier,
                    inc=1,
                    device_id={"dp": target, "fsdp": column},
                    device_id_type=MESH,
                )

    @pl.when(c == 0)
    def _():
        pl.semaphore_signal(barrier, inc=1, device_id={"fsdp": sibling}, device_id_type=MESH)

    pl.semaphore_wait(barrier, 2 * n_dp - 1 + c)

    @pl.when(c == 1)
    def _():
        pl.semaphore_signal(ready_sem, inc=1, device_id={"fsdp": sibling}, device_id_type=MESH)

    key_copies = []
    for k in range(n_dp):
        target = lax.rem(me + k, n_dp)
        for side, (column, lo) in enumerate(((f, own_lo), (peer, peer_lo))):
            src = ksend.at[target, :, pl.ds(lo, window)]
            dst = kbuf.at[x, me]
            if k == 0 and side == 0:
                copy = pltpu.make_async_copy(src, dst, key_recv_sem.at[side, k])
            else:
                copy = pltpu.make_async_remote_copy(
                    src_ref=src,
                    dst_ref=dst,
                    send_sem=key_send_sem.at[side, k],
                    recv_sem=key_recv_sem.at[side, k],
                    device_id={"dp": target, "fsdp": column},
                    device_id_type=MESH,
                )
            copy.start()
            key_copies.append(copy)

    @pl.when(c == 0)
    def _():
        pl.semaphore_wait(ready_sem, 1)

    shared = {}
    for s in (0, 1, layers, layers + 1, *range(2, layers)):
        shared[s] = pltpu.make_async_remote_copy(
            src_ref=sources[s],
            dst_ref=targets[s].at[pl.ds(base, rows_dev), :],
            send_sem=weight_sem.at[1, s],
            recv_sem=weight_sem.at[2, s],
            device_id={"fsdp": sibling},
            device_id_type=MESH,
        )
        shared[s].start()

    def have_weights(s):
        local_copies[s].wait()
        shared[s].wait_recv()

    pending = []

    def to_peer(src, dst, sems):
        copy = pltpu.make_async_remote_copy(
            src_ref=src,
            dst_ref=dst,
            send_sem=sems.at[0],
            recv_sem=sems.at[1],
            device_id={"fsdp": peer},
            device_id_type=MESH,
        )
        copy.start()
        pending.append(copy)
        return copy

    chunks = psend.shape[1]
    part_rows = rows // chunks
    part_images = 2 * images // chunks
    key_copies[0].wait()
    for copy in key_copies[1:]:
        copy.wait_recv()
    half_images = images // chunks
    entries = [
        kbuf[:, j * half_images : (j + 1) * half_images]
        .astype(jnp.float32)
        .reshape(2 * part_rows, window)
        .astype(jnp.bfloat16)
        for j in range(chunks)
    ]
    copies = [None] * chunks
    mines = [None] * chunks

    def settle(l, j):
        copies[j].wait_recv()
        full = mines[j] + precv[l, j].astype(jnp.float32)
        return jnp.maximum(full, 0.0).astype(jnp.bfloat16)

    for l in range(layers - 1):
        have_weights(l)
        for j in range(chunks):
            if l > 0:
                entries[j] = settle(l - 1, j)
            theirs = jnp.dot(
                entries[j], w[l, :, pl.ds(peer_lo, window)], preferred_element_type=jnp.float32
            )
            psend[l, j] = theirs.astype(jnp.bfloat16)
            copies[j] = to_peer(psend.at[l, j], precv.at[l, j], layer_sem.at[l, j])
            mines[j] = jnp.dot(
                entries[j], w[l, :, pl.ds(own_lo, window)], preferred_element_type=jnp.float32
            )

    have_weights(layers)
    have_weights(layers + 1)
    wides, parts = [None] * chunks, [None] * chunks
    for j in range(chunks):
        entry = settle(layers - 2, j)
        wides[j] = entry.astype(jnp.float32).reshape(part_images, positions, window)
        pooled = (jnp.sum(wides[j], axis=1) * (1.0 / positions)).astype(jnp.bfloat16)
        parts[j] = jnp.dot(pooled, red[...], preferred_element_type=jnp.float32)
        se_send[j] = parts[j]
        copies[j] = to_peer(se_send.at[j], se_recv.at[j], se_sem.at[j])

    have_weights(layers - 1)
    for j in range(chunks):
        copies[j].wait_recv()
        squeeze_act = jnp.maximum(parts[j] + se_recv[j], 0.0).astype(jnp.bfloat16)
        excite = jax.nn.sigmoid(
            lax.dot_general(
                squeeze_act, exp[...], (((1,), (1,)), ((), ())), preferred_element_type=jnp.float32
            )
        )
        scaled = (wides[j] * excite[:, None, :]).astype(jnp.bfloat16)
        both = jnp.dot(
            scaled.reshape(2 * part_rows, window), w[layers - 1], preferred_element_type=jnp.float32
        )
        low, high = both[:part_rows], both[part_rows:]
        last_send[j] = jnp.where(x == 0, high, low).astype(jnp.bfloat16)
        copies[j] = to_peer(last_send.at[j], last_recv.at[j], last_sem.at[j])
        mines[j] = jnp.where(x == 0, low, high)
    for j in range(chunks):
        copies[j].wait_recv()
        mines[j] = mines[j] + last_recv[j].astype(jnp.float32)
    count = images * positions
    mean_rows = sum(jnp.sum(mine, axis=0, keepdims=True) for mine in mines) / count
    squares = sum(jnp.sum(mine * mine, axis=0, keepdims=True) for mine in mines) / count
    scale_rows = lax.rsqrt(squares - mean_rows * mean_rows + epsilon) * gain_ref[...].reshape(
        1, channels
    )
    bias_rows = bias_ref[...].reshape(1, channels)
    for j in range(chunks):
        normed = (mines[j] - mean_rows) * scale_rows + bias_rows
        nsend[j * half_images : (j + 1) * half_images] = normed.reshape(
            half_images, positions, channels
        ).astype(jnp.bfloat16)

    back_copies = []
    for k in range(1, n_dp):
        target = lax.rem(me + k, n_dp)
        copy = pltpu.make_async_remote_copy(
            src_ref=nsend.at[target],
            dst_ref=nrecv.at[me],
            send_sem=back_send_sem.at[k - 1],
            recv_sem=back_recv_sem.at[k - 1],
            device_id={"dp": target},
            device_id_type=MESH,
        )
        copy.start()
        back_copies.append(copy)
    nrecv[me] = nsend[me]
    for copy in back_copies:
        copy.wait_recv()
    for i in range(images):
        out_ref[i] = nrecv[dests[i]]
    for copy in key_copies[1:] + list(shared.values()) + pending + back_copies:
        copy.wait_send()


def local_fused(n_dp, keys, residual, se_reduce, se_expand, conv_weight, bn_gain, bn_bias, shuffle, unshuffle):
    images, positions, channels = keys.shape
    layers, rows_dev, _ = conv_weight.shape
    units = se_reduce.shape[1]
    chunks = 4
    rows = images * positions
    half = 2 * rows_dev
    window = -(-half // lane) * lane
    bf16, f32 = jnp.bfloat16, jnp.float32
    vmem = pl.BlockSpec(memory_space=pltpu.VMEM)
    anywhere = pl.BlockSpec(memory_space=pl.ANY)
    dma = pltpu.SemaphoreType.DMA
    normed = pl.pallas_call(
        functools.partial(fused_kernel, n_dp, images, positions),
        out_shape=jax.ShapeDtypeStruct((images, positions, channels), bf16),
        in_specs=[anywhere] * 4 + [vmem] * 2 + [pl.BlockSpec(memory_space=pltpu.SMEM)],
        out_specs=vmem,
        scratch_shapes=[
            pltpu.VMEM((layers, window, channels), bf16),
            pltpu.VMEM((window, units), bf16),
            pltpu.VMEM((window, units), bf16),
            pltpu.VMEM((2, images, positions, window), bf16),
            pltpu.VMEM((layers - 1, chunks, 2 * rows // chunks, window), bf16),
            pltpu.VMEM((layers - 1, chunks, 2 * rows // chunks, window), bf16),
            pltpu.VMEM((chunks, 2 * images // chunks, units), f32),
            pltpu.VMEM((chunks, 2 * images // chunks, units), f32),
            pltpu.VMEM((chunks, rows // chunks, channels), bf16),
            pltpu.VMEM((chunks, rows // chunks, channels), bf16),
            pltpu.VMEM((images, positions, channels), bf16),
            pltpu.VMEM((n_dp, positions, channels), bf16),
            pltpu.VMEM((images, positions, channels), bf16),
            pltpu.VMEM((n_dp, positions, channels), bf16),
            dma,
            dma((2, n_dp)),
            dma((2, n_dp)),
            dma((3, layers + 2)),
            dma((layers - 1, chunks, 2)),
            dma((chunks, 2)),
            dma((chunks, 2)),
            dma((n_dp - 1,)),
            dma((n_dp - 1,)),
            pltpu.SemaphoreType.REGULAR,
        ],
        compiler_params=pltpu.CompilerParams(collective_id=0, has_side_effects=True),
        name="fused_encoder",
    )(
        keys,
        se_reduce,
        se_expand,
        conv_weight,
        bn_gain,
        bn_bias,
        shuffle,
    )
    encoded = jax.nn.relu(normed.astype(f32) + residual.astype(f32))
    return encoded.astype(bf16)


def solution(mesh):
    placed = (
        P(("dp", "fsdp"), None, None),
        P(("dp", "fsdp"), None, None),
        P("fsdp", None),
        P("fsdp", None),
        P(None, "fsdp", None),
        P(),
        P(),
        P(("dp", "fsdp")),
        P(("dp", "fsdp")),
    )
    n_dp, n_fsdp = mesh.shape["dp"], mesh.shape["fsdp"]

    def local(keys, *others):
        if n_fsdp == 4 and keys.shape[0] == n_dp:
            return local_fused(n_dp, keys, *others)
        return local_general(keys, *others)

    return jax.shard_map(
        local, mesh=mesh, in_specs=placed, out_specs=P(("dp", "fsdp"), None, None), check_vma=False
    )
```

```python
import functools

import jax
import jax.numpy as jnp
from jax import lax
from jax.experimental import pallas as pl
from jax.experimental.pallas import tpu as pltpu
from jax.sharding import PartitionSpec as P

epsilon = 1e-05
lane = 128
MESH = pl.DeviceIdType.MESH


def project_rows(flat, weight_rows):
    return jnp.dot(
        flat,
        lax.all_gather(weight_rows, "fsdp", axis=0, tiled=True),
        preferred_element_type=jnp.float32,
    )


def encode_block(batch_block, reduce_full, expand_full, conv_weight):
    images, positions, channels = batch_block.shape
    layers = conv_weight.shape[0]
    flat = batch_block.reshape(images * positions, channels)
    for layer in range(layers - 1):
        flat = jax.nn.relu(project_rows(flat, conv_weight[layer])).astype(jnp.bfloat16)
    entry = flat.reshape(images, positions, channels)
    pooled = jnp.mean(entry, axis=1, dtype=jnp.float32).astype(jnp.bfloat16)
    squeeze_act = jax.nn.relu(
        jnp.dot(pooled, reduce_full, preferred_element_type=jnp.float32)
    ).astype(jnp.bfloat16)
    excite = jax.nn.sigmoid(
        lax.dot_general(
            squeeze_act, expand_full, (((1,), (1,)), ((), ())), preferred_element_type=jnp.float32
        )
    )
    scaled = (entry * excite[:, None, :]).astype(jnp.bfloat16).reshape(images * positions, channels)
    projected = project_rows(scaled, conv_weight[layers - 1])
    return projected.reshape(images, positions, channels)


def local_general(keys, residual, se_reduce, se_expand, conv_weight, bn_gain, bn_bias, shuffle, unshuffle):
    images, positions, channels = keys.shape
    count = images * positions
    reduce_full, expand_full = (
        lax.all_gather(se_reduce, "fsdp", axis=0, tiled=True),
        lax.all_gather(se_expand, "fsdp", axis=0, tiled=True),
    )
    send_order = jnp.argsort(shuffle)
    back_order = jnp.argsort(send_order)
    outgoing = jnp.take(keys, send_order, axis=0)
    arrived = lax.all_to_all(outgoing, "dp", split_axis=0, concat_axis=0, tiled=True)
    projected = encode_block(arrived, reduce_full, expand_full, conv_weight)
    row_sums = jnp.sum(projected, axis=(0, 1))
    square_sums = jnp.sum(projected * projected, axis=(0, 1))
    mean_rows = row_sums / count
    variance = square_sums / count - mean_rows * mean_rows
    scale_rows = lax.rsqrt(variance + epsilon) * bn_gain
    normed_here = ((projected - mean_rows) * scale_rows + bn_bias).astype(jnp.bfloat16)
    returned = lax.all_to_all(normed_here, "dp", split_axis=0, concat_axis=0, tiled=True)
    normed = jnp.take(returned, back_order, axis=0)
    encoded = jax.nn.relu(normed.astype(jnp.float32) + residual.astype(jnp.float32))
    return encoded.astype(jnp.bfloat16)


def fused_kernel(
    n_dp,
    images,
    positions,
    keys_ref,
    reduce_ref,
    expand_ref,
    weight_ref,
    gain_ref,
    bias_ref,
    shuffle_ref,
    out_ref,
    w,
    red,
    exp,
    kbuf,
    psend,
    precv,
    se_send,
    se_recv,
    last_send,
    last_recv,
    keysv,
    ksend,
    nsend,
    nrecv,
    key_sem,
    key_send_sem,
    key_recv_sem,
    weight_sem,
    layer_sem,
    se_sem,
    last_sem,
    back_send_sem,
    back_recv_sem,
    ready_sem,
):
    me = lax.axis_index("dp")
    f = lax.axis_index("fsdp")
    x, c = f // 2, f % 2
    sibling = 2 * x + (1 - c)
    peer = 2 * (1 - x) + c
    layers, rows_dev, channels = weight_ref.shape
    half = 2 * rows_dev
    window = kbuf.shape[3]
    pad = window - half
    rows = images * positions
    own_lo = pl.multiple_of(x * (channels - window), lane)
    peer_lo = pl.multiple_of((1 - x) * (channels - window), lane)
    base = pl.multiple_of(x * pad + c * rows_dev, 16)

    keys_local = pltpu.make_async_copy(keys_ref, keysv, key_sem)
    keys_local.start()
    sources = [weight_ref.at[l] for l in range(layers)] + [reduce_ref, expand_ref]
    targets = [w.at[l] for l in range(layers)] + [red, exp]
    local_copies = []
    for s, (src, dst) in enumerate(zip(sources, targets)):
        copy = pltpu.make_async_copy(src, dst.at[pl.ds(base, rows_dev), :], weight_sem.at[0, s])
        copy.start()
        local_copies.append(copy)

    zero_lo = pl.multiple_of((1 - x) * half, 16)
    for l in range(layers):
        w[l, pl.ds(zero_lo, pad), :] = jnp.zeros((pad, channels), w.dtype)
    red[pl.ds(zero_lo, pad), :] = jnp.zeros((pad, red.shape[1]), red.dtype)
    exp[pl.ds(zero_lo, pad), :] = jnp.zeros((pad, exp.shape[1]), exp.dtype)

    dests = [lax.div(shuffle_ref[i], images) for i in range(images)]
    keys_local.wait()
    for e in range(n_dp):
        chosen = jnp.int32(0)
        for i in range(images):
            chosen = jnp.where(dests[i] == e, i, chosen)
        ksend[e] = keysv[chosen]

    barrier = pltpu.get_barrier_semaphore()
    for k in range(n_dp):
        target = lax.rem(me + k, n_dp)
        for column in (f, peer):
            if k > 0 or column is peer:
                pl.semaphore_signal(
                    barrier,
                    inc=1,
                    device_id={"dp": target, "fsdp": column},
                    device_id_type=MESH,
                )

    @pl.when(c == 0)
    def _():
        pl.semaphore_signal(barrier, inc=1, device_id={"fsdp": sibling}, device_id_type=MESH)

    pl.semaphore_wait(barrier, 2 * n_dp - 1 + c)

    @pl.when(c == 1)
    def _():
        pl.semaphore_signal(ready_sem, inc=1, device_id={"fsdp": sibling}, device_id_type=MESH)

    key_copies = []
    for k in range(n_dp):
        target = lax.rem(me + k, n_dp)
        for side, (column, lo) in enumerate(((f, own_lo), (peer, peer_lo))):
            src = ksend.at[target, :, pl.ds(lo, window)]
            dst = kbuf.at[x, me]
            if k == 0 and side == 0:
                copy = pltpu.make_async_copy(src, dst, key_recv_sem.at[side, k])
            else:
                copy = pltpu.make_async_remote_copy(
                    src_ref=src,
                    dst_ref=dst,
                    send_sem=key_send_sem.at[side, k],
                    recv_sem=key_recv_sem.at[side, k],
                    device_id={"dp": target, "fsdp": column},
                    device_id_type=MESH,
                )
            copy.start()
            key_copies.append(copy)

    @pl.when(c == 0)
    def _():
        pl.semaphore_wait(ready_sem, 1)

    shared = {}
    for s in (0, 1, layers, layers + 1, *range(2, layers)):
        shared[s] = pltpu.make_async_remote_copy(
            src_ref=sources[s],
            dst_ref=targets[s].at[pl.ds(base, rows_dev), :],
            send_sem=weight_sem.at[1, s],
            recv_sem=weight_sem.at[2, s],
            device_id={"fsdp": sibling},
            device_id_type=MESH,
        )
        shared[s].start()

    def have_weights(s):
        local_copies[s].wait()
        shared[s].wait_recv()

    pending = []

    def to_peer(src, dst, sems):
        copy = pltpu.make_async_remote_copy(
            src_ref=src,
            dst_ref=dst,
            send_sem=sems.at[0],
            recv_sem=sems.at[1],
            device_id={"fsdp": peer},
            device_id_type=MESH,
        )
        copy.start()
        pending.append(copy)
        return copy

    chunks = psend.shape[1]
    part_rows = rows // chunks
    part_images = 2 * images // chunks
    key_copies[0].wait()
    for copy in key_copies[1:]:
        copy.wait_recv()
    half_images = images // chunks
    entries = [
        kbuf[:, j * half_images : (j + 1) * half_images]
        .astype(jnp.float32)
        .reshape(2 * part_rows, window)
        .astype(jnp.bfloat16)
        for j in range(chunks)
    ]
    copies = [None] * chunks
    mines = [None] * chunks

    def settle(l, j):
        copies[j].wait_recv()
        full = mines[j] + precv[l, j].astype(jnp.float32)
        return jnp.maximum(full, 0.0).astype(jnp.bfloat16)

    def own_part(l, j):
        return jnp.dot(
            entries[j], w[l, :, pl.ds(own_lo, window)], preferred_element_type=jnp.float32
        )

    for l in range(layers - 1):
        have_weights(l)
        for j in range(chunks):
            if l > 0:
                entries[j] = settle(l - 1, j)
            theirs = jnp.dot(
                entries[j], w[l, :, pl.ds(peer_lo, window)], preferred_element_type=jnp.float32
            )
            psend[l, j] = theirs.astype(jnp.bfloat16)
            copies[j] = to_peer(psend.at[l, j], precv.at[l, j], layer_sem.at[l, j])
            if l > 0:
                mines[j] = own_part(l, j)
        if l == 0:
            mines = [own_part(l, j) for j in range(chunks)]

    have_weights(layers)
    have_weights(layers + 1)
    wides, parts = [None] * chunks, [None] * chunks
    for j in range(chunks):
        entry = settle(layers - 2, j)
        wides[j] = entry.astype(jnp.float32).reshape(part_images, positions, window)
        pooled = (jnp.sum(wides[j], axis=1) * (1.0 / positions)).astype(jnp.bfloat16)
        parts[j] = jnp.dot(pooled, red[...], preferred_element_type=jnp.float32)
        se_send[j] = parts[j]
        copies[j] = to_peer(se_send.at[j], se_recv.at[j], se_sem.at[j])

    have_weights(layers - 1)
    for j in range(chunks):
        copies[j].wait_recv()
        squeeze_act = jnp.maximum(parts[j] + se_recv[j], 0.0).astype(jnp.bfloat16)
        excite = jax.nn.sigmoid(
            lax.dot_general(
                squeeze_act, exp[...], (((1,), (1,)), ((), ())), preferred_element_type=jnp.float32
            )
        )
        scaled = (wides[j] * excite[:, None, :]).astype(jnp.bfloat16)
        both = jnp.dot(
            scaled.reshape(2 * part_rows, window), w[layers - 1], preferred_element_type=jnp.float32
        )
        low, high = both[:part_rows], both[part_rows:]
        last_send[j] = jnp.where(x == 0, high, low).astype(jnp.bfloat16)
        copies[j] = to_peer(last_send.at[j], last_recv.at[j], last_sem.at[j])
        mines[j] = jnp.where(x == 0, low, high)
    for j in range(chunks):
        copies[j].wait_recv()
        mines[j] = mines[j] + last_recv[j].astype(jnp.float32)
    count = images * positions
    mean_rows = sum(jnp.sum(mine, axis=0, keepdims=True) for mine in mines) / count
    squares = sum(jnp.sum(mine * mine, axis=0, keepdims=True) for mine in mines) / count
    scale_rows = lax.rsqrt(squares - mean_rows * mean_rows + epsilon) * gain_ref[...].reshape(
        1, channels
    )
    bias_rows = bias_ref[...].reshape(1, channels)
    for j in range(chunks):
        normed = (mines[j] - mean_rows) * scale_rows + bias_rows
        nsend[j * half_images : (j + 1) * half_images] = normed.reshape(
            half_images, positions, channels
        ).astype(jnp.bfloat16)

    back_copies = []
    for k in range(1, n_dp):
        target = lax.rem(me + k, n_dp)
        copy = pltpu.make_async_remote_copy(
            src_ref=nsend.at[target],
            dst_ref=nrecv.at[me],
            send_sem=back_send_sem.at[k - 1],
            recv_sem=back_recv_sem.at[k - 1],
            device_id={"dp": target},
            device_id_type=MESH,
        )
        copy.start()
        back_copies.append(copy)
    nrecv[me] = nsend[me]
    for copy in back_copies:
        copy.wait_recv()
    for i in range(images):
        out_ref[i] = nrecv[dests[i]]
    for copy in key_copies[1:] + list(shared.values()) + pending + back_copies:
        copy.wait_send()


def local_fused(n_dp, keys, residual, se_reduce, se_expand, conv_weight, bn_gain, bn_bias, shuffle, unshuffle):
    images, positions, channels = keys.shape
    layers, rows_dev, _ = conv_weight.shape
    units = se_reduce.shape[1]
    chunks = 4
    rows = images * positions
    half = 2 * rows_dev
    window = -(-half // lane) * lane
    bf16, f32 = jnp.bfloat16, jnp.float32
    vmem = pl.BlockSpec(memory_space=pltpu.VMEM)
    anywhere = pl.BlockSpec(memory_space=pl.ANY)
    dma = pltpu.SemaphoreType.DMA
    normed = pl.pallas_call(
        functools.partial(fused_kernel, n_dp, images, positions),
        out_shape=jax.ShapeDtypeStruct((images, positions, channels), bf16),
        in_specs=[anywhere] * 4 + [vmem] * 2 + [pl.BlockSpec(memory_space=pltpu.SMEM)],
        out_specs=vmem,
        scratch_shapes=[
            pltpu.VMEM((layers, window, channels), bf16),
            pltpu.VMEM((window, units), bf16),
            pltpu.VMEM((window, units), bf16),
            pltpu.VMEM((2, images, positions, window), bf16),
            pltpu.VMEM((layers - 1, chunks, 2 * rows // chunks, window), bf16),
            pltpu.VMEM((layers - 1, chunks, 2 * rows // chunks, window), bf16),
            pltpu.VMEM((chunks, 2 * images // chunks, units), f32),
            pltpu.VMEM((chunks, 2 * images // chunks, units), f32),
            pltpu.VMEM((chunks, rows // chunks, channels), bf16),
            pltpu.VMEM((chunks, rows // chunks, channels), bf16),
            pltpu.VMEM((images, positions, channels), bf16),
            pltpu.VMEM((n_dp, positions, channels), bf16),
            pltpu.VMEM((images, positions, channels), bf16),
            pltpu.VMEM((n_dp, positions, channels), bf16),
            dma,
            dma((2, n_dp)),
            dma((2, n_dp)),
            dma((3, layers + 2)),
            dma((layers - 1, chunks, 2)),
            dma((chunks, 2)),
            dma((chunks, 2)),
            dma((n_dp - 1,)),
            dma((n_dp - 1,)),
            pltpu.SemaphoreType.REGULAR,
        ],
        compiler_params=pltpu.CompilerParams(collective_id=0, has_side_effects=True),
        name="fused_encoder",
    )(
        keys,
        se_reduce,
        se_expand,
        conv_weight,
        bn_gain,
        bn_bias,
        shuffle,
    )
    encoded = jax.nn.relu(normed.astype(f32) + residual.astype(f32))
    return encoded.astype(bf16)


def solution(mesh):
    placed = (
        P(("dp", "fsdp"), None, None),
        P(("dp", "fsdp"), None, None),
        P("fsdp", None),
        P("fsdp", None),
        P(None, "fsdp", None),
        P(),
        P(),
        P(("dp", "fsdp")),
        P(("dp", "fsdp")),
    )
    n_dp, n_fsdp = mesh.shape["dp"], mesh.shape["fsdp"]

    def local(keys, *others):
        if n_fsdp == 4 and keys.shape[0] == n_dp:
            return local_fused(n_dp, keys, *others)
        return local_general(keys, *others)

    return jax.shard_map(
        local, mesh=mesh, in_specs=placed, out_specs=P(("dp", "fsdp"), None, None), check_vma=False
    )
```
